32 devices in a mesh: snap: 8 (over z, y), ord: 4 (over x, core).
Axes of the slice: x: 2, y: 2, z: 4, core: 2. Of those that a mesh axis runs over, the one named last changes fastest.
Arguments:
- images: bfloat16 [512, 256, 1024], P(('snap', 'ord')), may hold values from -8 to 8
- cycle_masks: int32 [512, 256], P('snap'), may hold values from 0 to 1, as said below
- weights: float32 [512], P('snap'), may hold values from 1 to 4
- inversion: float32 [128, 128], replicated, may hold values from -1 to 2
Outputs:
- kam: float32 [128, 256, 256], P('ord', 'snap')
The draws below stay inside these ranges and needn't reach their ends.
Inputs may be any that keep to these rules, and one draw needn't show every extreme that they name: `cycle_masks`: each entry is 0 or 1; the same 4 cycles, drawn from the seed, are 0 in every snapshot.
All inputs are finite; a program needn't handle non-finite values.
Results may differ from the reference program's by a relative error of at most 0.0015.
Values may be sent and summed in bfloat16 or wider, within the bound.
No kernel may reach another device: no remote copies, remote signals or barrier semaphores. Data moves between devices by JAX's collectives and lax.ppermute only.
A program may use at most 64 MiB of HBM per device.

```python
import math
import jax
import jax.numpy as jnp
from jax import lax

CYCLES = 256
ANGLES = 1024
ORDERS = 128
DEAD_CYCLES = 4
SNAP_DEV = 16
SNAPSHOTS = 512


def draw_images(key, part):
    cycle_gain = jax.random.uniform(jax.random.fold_in(key, 21), (1, CYCLES, 1), jnp.float32, 0.3, 1.0)
    noise = jax.random.normal(jax.random.fold_in(key, 29), (SNAPSHOTS, CYCLES, ANGLES), jnp.float32)
    common = jax.random.normal(jax.random.fold_in(key, 31), (SNAPSHOTS, 1, ANGLES), jnp.float32)
    values = 0.8 * noise + cycle_gain * common
    return jnp.clip(values, -8.0, 8.0).astype(jnp.bfloat16)


def draw_cycle_masks(key, part):
    threshold = jax.random.randint(jax.random.fold_in(key, 3), (SNAPSHOTS, 1), 300, 1001)
    alive_draw = jax.random.randint(jax.random.fold_in(key, 4), (SNAPSHOTS, CYCLES), 0, 1000) < threshold
    radius = jax.random.randint(jax.random.fold_in(key, 6), (SNAPSHOTS, 1), 0, CYCLES // 2)
    cycle_index = jnp.arange(CYCLES, dtype=jnp.int32)[None, :]
    outside = cycle_index >= radius
    cycle_rank = jax.random.permutation(jax.random.fold_in(key, 5), CYCLES)
    blocked = cycle_rank < DEAD_CYCLES
    alive = jnp.logical_and(alive_draw, outside).astype(jnp.int32)
    return jnp.where(blocked[None, :], 0, alive).astype(jnp.int32)


def draw_inversion(key, part):
    noise = jax.random.uniform(jax.random.fold_in(key, 7), (ORDERS, ORDERS), jnp.float32, -1.0, 1.0) * 0.6
    return jnp.eye(ORDERS, dtype=jnp.float32) + noise / jnp.sqrt(ORDERS * 1.0)


def shard_levels(key, dims, split, least, high):
    gain, own = 1.0, jax.random.fold_in(key, 6)
    for position, blocks in split:
        draws = jnp.exp(jax.random.uniform(jax.random.fold_in(own, position), (blocks,), jnp.float32, least / len(split), high / len(split)))
        gain = gain * jnp.repeat(draws, dims[position] // blocks).reshape([-1 if axis == position else 1 for axis in range(len(dims))])
    return gain


def setup_inputs(seed: int = 0) -> dict:
    keys = jax.random.split(jax.random.key(seed), 5)
    images = draw_images(jax.random.fold_in(keys[4], 71), 0)
    cycle_masks = draw_cycle_masks(jax.random.fold_in(keys[4], 71), 0)
    weights = jnp.clip(1.0 + 3.0 * jax.random.uniform(keys[2], (SNAPSHOTS,), jnp.float32) ** shard_levels(keys[2], (SNAPSHOTS,), ((0, 8),), -0.2, 0.2), 1.0, 4.0)
    inversion = draw_inversion(jax.random.fold_in(keys[4], 71), 0)
    return {"images": images, "cycle_masks": cycle_masks, "weights": weights, "inversion": inversion}


def make_table(orders, angles):
    order_index = jnp.arange(orders, dtype=jnp.int32)
    angle_index = jnp.arange(angles, dtype=jnp.int32)
    phase_index = order_index[:, None] * angle_index[None, :] % angles
    radians = phase_index.astype(jnp.float32) * (2.0 * math.pi / angles)
    norming = math.sqrt(2.0 / angles)
    return jnp.concatenate([jnp.cos(radians) * norming, -jnp.sin(radians) * norming], axis=0).astype(jnp.bfloat16)

def reference(images, cycle_masks, weights, inversion):
    dft_table = make_table(ORDERS, ANGLES)
    table_cols = dft_table.astype(jnp.float32).T
    block_count = images.shape[0] // SNAP_DEV

    def accumulate(state_pair, block_index):
        gram_sum, pair_count = state_pair
        first_row = (block_index * SNAP_DEV).astype(jnp.int32)
        image_block = lax.dynamic_slice_in_dim(images, first_row, SNAP_DEV, 0)
        mask_block = lax.dynamic_slice_in_dim(cycle_masks, first_row, SNAP_DEV, 0).astype(jnp.float32)
        weight_block = lax.dynamic_slice_in_dim(weights, first_row, SNAP_DEV, 0).astype(jnp.float32)
        flat_rows = image_block.reshape(SNAP_DEV * CYCLES, ANGLES).astype(jnp.float32)
        spectra = jnp.dot(flat_rows, table_cols, precision=lax.Precision.HIGHEST)
        coeffs = spectra.T.reshape(2 * ORDERS, SNAP_DEV, CYCLES)
        coeffs = (coeffs * mask_block[None]).astype(jnp.bfloat16).reshape(2, ORDERS, SNAP_DEV, CYCLES)
        weighted = (coeffs.astype(jnp.float32) * weight_block[None, None, :, None]).astype(jnp.bfloat16)
        gram_sum = gram_sum + jnp.einsum('rlsq,rlsp->lqp', weighted.astype(jnp.float32), coeffs.astype(jnp.float32), precision=lax.Precision.HIGHEST)
        masked_weight = mask_block * weight_block[:, None]
        pair_count = pair_count + jnp.einsum('sq,sp->qp', masked_weight, mask_block, precision=lax.Precision.HIGHEST)
        return ((gram_sum, pair_count), None)
    initial = (jnp.zeros((ORDERS, CYCLES, CYCLES), jnp.float32), jnp.zeros((CYCLES, CYCLES), jnp.float32))
    (gram_sum, pair_count), _ = lax.scan(accumulate, initial, jnp.arange(block_count, dtype=jnp.int32))
    correl = gram_sum / jnp.maximum(pair_count, 1.0)[None]
    kam = jnp.dot(inversion, correl.reshape(ORDERS, CYCLES * CYCLES), precision=lax.Precision.HIGHEST)
    return kam.reshape(ORDERS, CYCLES, CYCLES)
```

```python
import math

import jax
import jax.numpy as jnp
import numpy as np
from jax import lax
from jax.sharding import Mesh, PartitionSpec as P

HALVES = 2
SNAP = ("high", "low")
ORD = ("x", "core")
GRAM_SCALE = 2.0**33
KAM_SCALE = 2.0**38


def make_table(orders, angles):
    order_index = np.arange(orders)[:, None]
    angle_index = np.arange(angles)[None, :]
    phase_index = (order_index * angle_index) % angles
    radians = phase_index.astype(np.float32) * np.float32(2.0 * math.pi / angles)
    norming = np.float32(math.sqrt(2.0 / angles))
    return np.stack([np.cos(radians) * norming, -np.sin(radians) * norming])


def encode(value, scale):
    scaled = value * scale
    return (scaled * jnp.abs(scaled)).astype(jnp.bfloat16)


def decode(code, scale):
    code = code.astype(jnp.float32)
    root = jnp.sqrt(jnp.abs(code)) * (1.0 / scale)
    return jnp.where(code < 0, -root, root)


def swap(value, axis, size, shift):
    return lax.ppermute(value, axis, [(at, (at + shift) % size) for at in range(size)])


def on_device(images, cycle_masks, weights, inversion):
    snap_dev, cycles, angles = images.shape
    orders = inversion.shape[0]
    low_size, x_size, core_size = (lax.axis_size(name) for name in ("low", "x", "core"))
    ord_size = x_size * core_size
    snap_size = HALVES * low_size
    x_index, core_index = lax.axis_index("x"), lax.axis_index("core")
    ord_index = x_index * core_size + core_index
    group = low_size * ord_size
    owned = orders // group
    rows = cycles // snap_size
    chip_orders = orders // x_size
    out_orders = orders // ord_size

    masks = cycle_masks.astype(jnp.float32)
    counts = jnp.einsum("sq,sp->qp", masks * weights[:, None], masks, precision=lax.Precision.HIGHEST)
    weight_row = jnp.zeros((1, cycles), jnp.float32).at[0, : weights.shape[0]].set(weights)
    early = jnp.concatenate(
        [
            counts.reshape(snap_size, rows, cycles),
            jnp.broadcast_to(weight_row[None], (snap_size, 1, cycles)),
        ],
        axis=1,
    )
    early = lax.all_to_all(early, SNAP, split_axis=0, concat_axis=0, tiled=True)
    pair_count = early[:, :rows].sum(0)
    half = early.reshape(HALVES, low_size, rows + 1, cycles)
    half = lax.dynamic_index_in_dim(half, lax.axis_index("high"), 0, keepdims=False)
    weight_half = half[:, rows, : weights.shape[0]].reshape(group, snap_dev)

    own_masks = lax.dynamic_slice_in_dim(masks, ord_index * snap_dev, snap_dev, 0)
    table = make_table(orders, angles).reshape(2, ord_size, low_size, owned, angles)
    table = table.transpose(2, 1, 0, 3, 4).reshape(2 * orders, angles)
    table = jnp.asarray(table).astype(jnp.bfloat16)
    coeffs = jnp.einsum("ka,sqa->ksq", table, images, preferred_element_type=jnp.float32)
    coeffs = (coeffs * own_masks[None]).astype(jnp.bfloat16)
    coeffs = coeffs.reshape(group, 2, owned, snap_dev, cycles)
    arrived = lax.all_to_all(coeffs, ("low", "x", "core"), split_axis=0, concat_axis=0, tiled=True)
    weighted = arrived.astype(jnp.float32) * weight_half[:, None, None, :, None]
    gram = jnp.einsum(
        "drnsq,drnsp->nqp", weighted.astype(jnp.bfloat16), arrived, preferred_element_type=jnp.float32
    )
    gram = encode(gram, GRAM_SCALE).reshape(owned, snap_size, rows, cycles).transpose(1, 0, 2, 3)
    gram = lax.all_to_all(gram, SNAP, split_axis=0, concat_axis=0, tiled=True)
    gram = decode(gram, GRAM_SCALE).reshape(HALVES, low_size * owned, rows, cycles).sum(0)
    other = swap(encode(gram, GRAM_SCALE), "core", core_size, 1)
    other = decode(other, GRAM_SCALE)
    own_part = lax.dynamic_slice_in_dim(inversion, x_index * chip_orders, chip_orders, 1)
    own_part = own_part.reshape(orders, core_size, out_orders)
    mine = lax.dynamic_index_in_dim(own_part, core_index, 1, keepdims=False)
    theirs = lax.dynamic_index_in_dim(own_part, 1 - core_index, 1, keepdims=False)
    norm = 1.0 / jnp.maximum(pair_count, 1.0)
    total = 0.0
    for shift in reversed(range(x_size)):
        target = ((x_index + shift) % x_size * core_size + core_index) * out_orders
        kam = sum(
            jnp.einsum(
                "ln,nqp->lqp",
                lax.dynamic_slice_in_dim(part, target, out_orders, 0),
                value,
                precision=lax.Precision.HIGHEST,
            )
            for part, value in ((mine, gram), (theirs, other))
        )
        kam = kam * norm[None]
        if shift:
            kam = decode(swap(encode(kam, KAM_SCALE), "x", x_size, shift), KAM_SCALE)
        total = total + kam
    return total


def solution(mesh):
    snap_size, ord_size = mesh.shape["snap"], mesh.shape["ord"]
    fine = Mesh(
        mesh.devices.reshape(HALVES, snap_size // HALVES, ord_size // 2, 2), SNAP + ORD
    )
    placed = (P(SNAP + ORD, None, None), P(SNAP, None), P(SNAP), P())
    return jax.shard_map(
        on_device, mesh=fine, in_specs=placed, out_specs=P(ORD, SNAP, None), check_vma=False
    )
```

```python
import math

import jax
import jax.numpy as jnp
import numpy as np
from jax import lax
from jax.experimental import pallas as pl
from jax.experimental.pallas import tpu as pltpu
from jax.sharding import Mesh, PartitionSpec as P

HALVES = 2
SNAP = ("high", "low")
ORD = ("x", "core")
LANES = 128
STEP_SNAPS = 8
GROUP = ("low", "x", "core")
GRAM_SCALE = 2.0**33


def make_table(orders, angles):
    order_index = np.arange(orders)[:, None]
    angle_index = np.arange(angles)[None, :]
    phase_index = (order_index * angle_index) % angles
    radians = phase_index.astype(np.float32) * np.float32(2.0 * math.pi / angles)
    norming = np.float32(math.sqrt(2.0 / angles))
    return np.stack([np.cos(radians) * norming, -np.sin(radians) * norming])


def encode(value):
    scaled = value * GRAM_SCALE
    return (scaled * jnp.abs(scaled)).astype(jnp.bfloat16)


def decode(code):
    code = code.astype(jnp.float32)
    root = jnp.sqrt(jnp.abs(code)) * (1.0 / GRAM_SCALE)
    return jnp.where(code < 0, -root, root)


def dft_kernel(table_ref, mask_ref, image_ref, *refs):
    outs, held = refs[:-1], refs[-1]
    step = pl.program_id(0)
    count = table_ref.shape[0]
    snap_dev, size = mask_ref.shape[0], count // len(outs)
    for k in range(image_ref.shape[0]):
        snap = step * image_ref.shape[0] + k
        value = lax.dot_general(
            table_ref[...], image_ref[k], (((1,), (1,)), ((), ())), preferred_element_type=jnp.float32
        )
        value = value * mask_ref[pl.ds(snap, 1), :]
        for lane in range(held.shape[0]):
            lanes = slice(lane * LANES, (lane + 1) * LANES)
            held[lane, pl.ds(snap, count, stride=snap_dev), :] = value[:, lanes]

    @pl.when(step == pl.num_programs(0) - 1)
    def _():
        for chunk, out in enumerate(outs):
            for lane in range(held.shape[0]):
                lanes = slice(lane * LANES, (lane + 1) * LANES)
                whole = held[lane, pl.ds(chunk * size * snap_dev, size * snap_dev), :]
                out[:, :, lanes] = whole.astype(jnp.bfloat16).reshape(size, snap_dev, LANES)


def transform(table, masks, images, chunks):
    snap_dev, cycles, angles = images.shape
    count = table.shape[0]
    vmem = pl.BlockSpec(memory_space=pltpu.VMEM)
    out = jax.ShapeDtypeStruct((count // chunks, snap_dev, cycles), jnp.bfloat16)
    return pl.pallas_call(
        dft_kernel,
        grid=(snap_dev // STEP_SNAPS,),
        in_specs=[vmem, vmem, pl.BlockSpec((STEP_SNAPS, cycles, angles), lambda i: (i, 0, 0))],
        out_specs=[vmem] * chunks,
        out_shape=[out] * chunks,
        scratch_shapes=[pltpu.VMEM((cycles // LANES, count * snap_dev, LANES), jnp.float32)],
        compiler_params=pltpu.CompilerParams(vmem_limit_bytes=58 << 20),
    )(table, masks, images)


def swap(value, axis, size, shift):
    return lax.ppermute(value, axis, [(at, (at + shift) % size) for at in range(size)])


def at(value, index, axis=0):
    return lax.dynamic_index_in_dim(value, index, axis, keepdims=False)


def exchange(blocks, me, size):
    return [
        lax.ppermute(at(blocks, me ^ shift), SNAP, [(dev, dev ^ shift) for dev in range(size)])
        if shift
        else at(blocks, me)
        for shift in range(size)
    ]


def on_device(images, cycle_masks, weights, inversion):
    snap_dev, cycles, angles = images.shape
    orders = inversion.shape[0]
    low_size, x_size, core_size = (lax.axis_size(name) for name in GROUP)
    low, x_index, core_index = (lax.axis_index(name) for name in GROUP)
    ord_size = x_size * core_size
    snap_size = HALVES * low_size
    ord_index = x_index * core_size + core_index
    snap_index = lax.axis_index("high") * low_size + low
    group = low_size * ord_size
    owned = orders // group
    chunks = min(2, owned)
    part = owned // chunks
    rows = cycles // snap_size
    out_orders = orders // ord_size

    own_masks = lax.dynamic_slice_in_dim(cycle_masks, ord_index * snap_dev, snap_dev, 0)
    own_masks = own_masks.astype(jnp.float32)
    table = make_table(orders, angles).reshape(2, ord_size, low_size, chunks, part, angles)
    table = table.transpose(3, 2, 1, 0, 4, 5).reshape(2 * orders, angles)
    table = jnp.asarray(table).astype(jnp.bfloat16)

    coeffs = list(transform(table, own_masks, images, chunks))
    coeffs[0], cycle_masks, weights = lax.optimization_barrier((coeffs[0], cycle_masks, weights))
    arrived = []
    for chunk in range(chunks):
        with jax.named_scope(f"coefs{chunk}"):
            block = coeffs[chunk].reshape(group, 2 * part * snap_dev, cycles)
            block = lax.all_to_all(block, GROUP, split_axis=0, concat_axis=0, tiled=True)
            arrived.append(block.reshape(group, 2, part, snap_dev, cycles))

    masks = cycle_masks.astype(jnp.float32)
    counts = jnp.einsum("sq,sp->qp", masks * weights[:, None], masks, precision=lax.Precision.HIGHEST)
    weight_row = jnp.zeros((1, cycles), jnp.float32).at[0, : weights.shape[0]].set(weights)
    early = jnp.concatenate(
        [
            counts.reshape(snap_size, rows, cycles),
            jnp.broadcast_to(weight_row[None], (snap_size, 1, cycles)),
        ],
        axis=1,
    )
    blocks = exchange(early, snap_index, snap_size)
    pair_count = sum(block[:rows] for block in blocks)
    weight_half = jnp.stack([block[rows, : weights.shape[0]] for block in blocks[:low_size]])
    weight_half = jnp.stack([at(weight_half, low ^ k) for k in range(low_size)])
    weight_half = weight_half.reshape(group, snap_dev)

    own_rows = lax.dynamic_slice_in_dim(inversion, ord_index * out_orders, out_orders, 0)
    own_rows = own_rows.reshape(out_orders, x_size, core_size, low_size, chunks, part)

    def contract(value, chunk, x_from, core_from, crossed):
        picked = at(at(own_rows[:, :, :, :, chunk], x_from, 1), core_from, 1)
        if crossed:
            picked = jnp.stack([at(picked, low ^ k, 1) for k in range(low_size)], axis=1)
        return jnp.einsum(
            "ln,nqp->lqp",
            picked.reshape(out_orders, low_size * part),
            value,
            precision=lax.Precision.HIGHEST,
        )

    total = 0.0
    for chunk in range(chunks):
        weighted = arrived[chunk].astype(jnp.float32) * weight_half[:, None, None, :, None]
        gram = jnp.einsum(
            "drnsq,drnsp->nqp",
            weighted.astype(jnp.bfloat16),
            arrived[chunk],
            preferred_element_type=jnp.float32,
        )
        gram = encode(gram).reshape(part, snap_size, rows, cycles).transpose(1, 0, 2, 3)
        crossed = chunk < chunks - 1
        if crossed:
            got = exchange(gram, snap_index, snap_size)
            gram = jnp.concatenate(
                [decode(got[k]) + decode(got[k + low_size]) for k in range(low_size)]
            )
        else:
            gram = lax.all_to_all(gram, SNAP, split_axis=0, concat_axis=0, tiled=True)
            gram = decode(gram).reshape(HALVES, low_size * part, rows, cycles).sum(0)
        code = encode(gram)
        total = total + contract(gram, chunk, x_index, core_index, crossed)
        for shift in range(x_size):
            x_from = (x_index - shift) % x_size
            seen = swap(code, "x", x_size, shift) if shift else code
            if shift:
                total = total + contract(decode(seen), chunk, x_from, core_index, crossed)
            far = swap(seen, "core", core_size, 1)
            total = total + contract(decode(far), chunk, x_from, 1 - core_index, crossed)
    return total * (1.0 / jnp.maximum(pair_count, 1.0))[None]


def solution(mesh):
    snap_size, ord_size = mesh.shape["snap"], mesh.shape["ord"]
    fine = Mesh(
        mesh.devices.reshape(HALVES, snap_size // HALVES, ord_size // 2, 2), SNAP + ORD
    )
    placed = (P(SNAP + ORD, None, None), P(SNAP, None), P(SNAP), P())
    return jax.shard_map(
        on_device, mesh=fine, in_specs=placed, out_specs=P(ORD, SNAP, None), check_vma=False
    )
```

```python
import math

import jax
import jax.numpy as jnp
import numpy as np
from jax import lax
from jax.experimental import pallas as pl
from jax.experimental.pallas import tpu as pltpu
from jax.sharding import Mesh, PartitionSpec as P

HALVES = 2
SNAP = ("high", "low")
ORD = ("x", "core")
LANES = 128
STEP_SNAPS = 8
GROUP = ("low", "x", "core")
GRAM_SCALE = 2.0**33


def make_table(orders, angles):
    order_index = np.arange(orders)[:, None]
    angle_index = np.arange(angles)[None, :]
    phase_index = (order_index * angle_index) % angles
    radians = phase_index.astype(np.float32) * np.float32(2.0 * math.pi / angles)
    norming = np.float32(math.sqrt(2.0 / angles))
    return np.stack([np.cos(radians) * norming, -np.sin(radians) * norming])


def encode(value):
    scaled = value * GRAM_SCALE
    return (scaled * jnp.abs(scaled)).astype(jnp.bfloat16)


def decode(code):
    code = code.astype(jnp.float32)
    root = jnp.sqrt(jnp.abs(code)) * (1.0 / GRAM_SCALE)
    return jnp.where(code < 0, -root, root)


def dft_kernel(first_ref, table_ref, mask_ref, image_ref, *refs):
    outs, held = refs[:-1], refs[-1]
    step = pl.program_id(0)
    count = table_ref.shape[0]
    snap_dev, size = outs[0].shape[1], count // len(outs)
    for k in range(image_ref.shape[0]):
        snap = step * image_ref.shape[0] + k
        value = lax.dot_general(
            table_ref[...], image_ref[k], (((1,), (1,)), ((), ())), preferred_element_type=jnp.float32
        )
        value = value * mask_ref[pl.ds(first_ref[0] + snap, 1), :].astype(jnp.float32)
        for lane in range(held.shape[0]):
            lanes = slice(lane * LANES, (lane + 1) * LANES)
            held[lane, pl.ds(snap, count, stride=snap_dev), :] = value[:, lanes]

    @pl.when(step == pl.num_programs(0) - 1)
    def _():
        for chunk, out in enumerate(outs):
            for lane in range(held.shape[0]):
                lanes = slice(lane * LANES, (lane + 1) * LANES)
                whole = held[lane, pl.ds(chunk * size * snap_dev, size * snap_dev), :]
                out[:, :, lanes] = whole.astype(jnp.bfloat16).reshape(size, snap_dev, LANES)


def transform(first, table, masks, images, chunks):
    snap_dev, cycles, angles = images.shape
    count = table.shape[0]
    vmem = pl.BlockSpec(memory_space=pltpu.VMEM)
    out = jax.ShapeDtypeStruct((count // chunks, snap_dev, cycles), jnp.bfloat16)
    return pl.pallas_call(
        dft_kernel,
        grid=(snap_dev // STEP_SNAPS,),
        in_specs=[
            pl.BlockSpec(memory_space=pltpu.SMEM),
            vmem,
            vmem,
            pl.BlockSpec((STEP_SNAPS, cycles, angles), lambda i: (i, 0, 0)),
        ],
        out_specs=[vmem] * chunks,
        out_shape=[out] * chunks,
        scratch_shapes=[pltpu.VMEM((cycles // LANES, count * snap_dev, LANES), jnp.float32)],
        compiler_params=pltpu.CompilerParams(vmem_limit_bytes=58 << 20),
    )(first, table, masks, images)


def swap(value, axis, size, shift):
    return lax.ppermute(value, axis, [(at, (at + shift) % size) for at in range(size)])


def at(value, index, axis=0):
    return lax.dynamic_index_in_dim(value, index, axis, keepdims=False)


def exchange(blocks, me, size):
    return [
        lax.ppermute(at(blocks, me ^ shift), SNAP, [(dev, dev ^ shift) for dev in range(size)])
        if shift
        else at(blocks, me)
        for shift in range(size)
    ]


def on_device(images, cycle_masks, weights, inversion):
    snap_dev, cycles, angles = images.shape
    orders = inversion.shape[0]
    low_size, x_size, core_size = (lax.axis_size(name) for name in GROUP)
    low, x_index, core_index = (lax.axis_index(name) for name in GROUP)
    ord_size = x_size * core_size
    snap_size = HALVES * low_size
    ord_index = x_index * core_size + core_index
    snap_index = lax.axis_index("high") * low_size + low
    group = low_size * ord_size
    owned = orders // group
    chunks = min(2, owned)
    part = owned // chunks
    rows = cycles // snap_size
    out_orders = orders // ord_size

    table = make_table(orders, angles).reshape(2, ord_size, low_size, chunks, part, angles)
    table = table.transpose(3, 2, 1, 0, 4, 5).reshape(2 * orders, angles)
    table = jnp.asarray(table).astype(jnp.bfloat16)

    first = jnp.reshape(ord_index * snap_dev, (1,)).astype(jnp.int32)
    coeffs = list(transform(first, table, cycle_masks, images, chunks))
    coeffs[0], cycle_masks, weights = lax.optimization_barrier((coeffs[0], cycle_masks, weights))
    arrived = []
    for chunk in range(chunks):
        with jax.named_scope(f"coefs{chunk}"):
            block = coeffs[chunk].reshape(group, 2 * part * snap_dev, cycles)
            block = lax.all_to_all(block, GROUP, split_axis=0, concat_axis=0, tiled=True)
            arrived.append(block.reshape(group, 2, part, snap_dev, cycles))

    masks = cycle_masks.astype(jnp.float32)
    counts = jnp.einsum("sq,sp->qp", masks * weights[:, None], masks, precision=lax.Precision.HIGHEST)
    weight_row = jnp.zeros((1, cycles), jnp.float32).at[0, : weights.shape[0]].set(weights)
    early = jnp.concatenate(
        [
            counts.reshape(snap_size, rows, cycles),
            jnp.broadcast_to(weight_row[None], (snap_size, 1, cycles)),
        ],
        axis=1,
    )
    blocks = exchange(early, snap_index, snap_size)
    pair_count = sum(block[:rows] for block in blocks)
    weight_half = jnp.stack([block[rows, : weights.shape[0]] for block in blocks[:low_size]])
    weight_half = jnp.stack([at(weight_half, low ^ k) for k in range(low_size)])
    weight_half = weight_half.reshape(group, snap_dev)

    own_rows = lax.dynamic_slice_in_dim(inversion, ord_index * out_orders, out_orders, 0)
    own_rows = own_rows.reshape(out_orders, x_size, core_size, low_size, chunks, part)

    def contract(value, chunk, x_from, core_from, crossed):
        picked = at(at(own_rows[:, :, :, :, chunk], x_from, 1), core_from, 1)
        if crossed:
            picked = jnp.stack([at(picked, low ^ k, 1) for k in range(low_size)], axis=1)
        return jnp.einsum(
            "ln,nqp->lqp",
            picked.reshape(out_orders, low_size * part),
            value,
            precision=lax.Precision.HIGHEST,
        )

    total = 0.0
    for chunk in range(chunks):
        weighted = arrived[chunk].astype(jnp.float32) * weight_half[:, None, None, :, None]
        gram = jnp.einsum(
            "drnsq,drnsp->nqp",
            weighted.astype(jnp.bfloat16),
            arrived[chunk],
            preferred_element_type=jnp.float32,
        )
        gram = encode(gram).reshape(part, snap_size, rows, cycles).transpose(1, 0, 2, 3)
        crossed = chunk < chunks - 1
        if crossed:
            got = exchange(gram, snap_index, snap_size)
            gram = jnp.concatenate(
                [decode(got[k]) + decode(got[k + low_size]) for k in range(low_size)]
            )
        else:
            gram = lax.all_to_all(gram, SNAP, split_axis=0, concat_axis=0, tiled=True)
            gram = decode(gram).reshape(HALVES, low_size * part, rows, cycles).sum(0)
        code = encode(gram)
        total = total + contract(gram, chunk, x_index, core_index, crossed)
        for shift in range(x_size):
            x_from = (x_index - shift) % x_size
            seen = swap(code, "x", x_size, shift) if shift else code
            if shift:
                total = total + contract(decode(seen), chunk, x_from, core_index, crossed)
            far = swap(seen, "core", core_size, 1)
            total = total + contract(decode(far), chunk, x_from, 1 - core_index, crossed)
    return total * (1.0 / jnp.maximum(pair_count, 1.0))[None]


def solution(mesh):
    snap_size, ord_size = mesh.shape["snap"], mesh.shape["ord"]
    fine = Mesh(
        mesh.devices.reshape(HALVES, snap_size // HALVES, ord_size // 2, 2), SNAP + ORD
    )
    placed = (P(SNAP + ORD, None, None), P(SNAP, None), P(SNAP), P())
    return jax.shard_map(
        on_device, mesh=fine, in_specs=placed, out_specs=P(ORD, SNAP, None), check_vma=False
    )
```

```python
import math

import jax
import jax.numpy as jnp
import numpy as np
from jax import lax
from jax.experimental import pallas as pl
from jax.experimental.pallas import tpu as pltpu
from jax.sharding import Mesh, PartitionSpec as P

HALVES = 2
SNAP = ("high", "low")
ORD = ("x", "core")
LANES = 128
STEP_SNAPS = 8
GROUP = ("low", "x", "core")
GRAM_SCALE = 2.0**33


def make_table(orders, angles):
    order_index = np.arange(orders)[:, None]
    angle_index = np.arange(angles)[None, :]
    phase_index = (order_index * angle_index) % angles
    radians = phase_index.astype(np.float32) * np.float32(2.0 * math.pi / angles)
    norming = np.float32(math.sqrt(2.0 / angles))
    return np.stack([np.cos(radians) * norming, -np.sin(radians) * norming])


def encode(value):
    scaled = value * GRAM_SCALE
    return (scaled * jnp.abs(scaled)).astype(jnp.bfloat16)


def decode(code):
    code = code.astype(jnp.float32)
    root = jnp.sqrt(jnp.abs(code)) * (1.0 / GRAM_SCALE)
    return jnp.where(code < 0, -root, root)


def dft_kernel(first_ref, table_ref, mask_ref, image_ref, *refs):
    *direct, last, held = refs
    step = pl.program_id(0)
    snaps = image_ref.shape[0]
    size, snap_dev, cycles = last.shape
    lanes = [slice(start, start + LANES) for start in range(0, cycles, LANES)]
    for k in range(snaps):
        snap = step * snaps + k
        value = lax.dot_general(
            table_ref[...], image_ref[k], (((1,), (1,)), ((), ())), preferred_element_type=jnp.float32
        )
        value = value * mask_ref[pl.ds(first_ref[0] + snap, 1), :].astype(jnp.float32)
        for index, out in enumerate(direct):
            part = value[index * size : (index + 1) * size]
            out[:, k] = part.reshape(out.shape[0], out.shape[2], cycles).astype(jnp.bfloat16)
        for lane, cut in enumerate(lanes):
            held[lane, pl.ds(snap, size, stride=snap_dev), :] = value[len(direct) * size :, cut]

    @pl.when(step == pl.num_programs(0) - 1)
    def _():
        for lane, cut in enumerate(lanes):
            last[:, :, cut] = held[lane].astype(jnp.bfloat16).reshape(size, snap_dev, LANES)


def transform(first, table, masks, images, chunks, group):
    snap_dev, cycles, angles = images.shape
    size = table.shape[0] // chunks
    lines = size // group
    vmem = pl.BlockSpec(memory_space=pltpu.VMEM)
    direct = [jax.ShapeDtypeStruct((group, snap_dev, lines, cycles), jnp.bfloat16)] * (chunks - 1)
    return pl.pallas_call(
        dft_kernel,
        grid=(snap_dev // STEP_SNAPS,),
        in_specs=[
            pl.BlockSpec(memory_space=pltpu.SMEM),
            vmem,
            vmem,
            pl.BlockSpec((STEP_SNAPS, cycles, angles), lambda i: (i, 0, 0)),
        ],
        out_specs=[pl.BlockSpec((group, STEP_SNAPS, lines, cycles), lambda i: (0, i, 0, 0))]
        * len(direct)
        + [vmem],
        out_shape=direct + [jax.ShapeDtypeStruct((size, snap_dev, cycles), jnp.bfloat16)],
        scratch_shapes=[pltpu.VMEM((cycles // LANES, size * snap_dev, LANES), jnp.float32)],
        compiler_params=pltpu.CompilerParams(vmem_limit_bytes=58 << 20),
    )(first, table, masks, images)


def finish_kernel(factor_ref, before_ref, count_ref, *refs):
    codes, (out_ref, held) = refs[:-2], refs[-2:]
    out_orders, rows, cycles = out_ref.shape
    lanes = [slice(start, start + LANES) for start in range(0, cycles, LANES)]
    share = 1.0 / jnp.maximum(count_ref[...], 1.0)
    for row in range(rows):
        value = jnp.concatenate([decode(code_ref[row]) for code_ref in codes], axis=0)
        high = value.astype(jnp.bfloat16).astype(jnp.float32)
        value = jnp.dot(
            factor_ref[...],
            jnp.concatenate([high, value - high, high], axis=0).astype(jnp.bfloat16),
            preferred_element_type=jnp.float32,
        )
        value = (value + before_ref[row]) * share[row : row + 1]
        for lane, cut in enumerate(lanes):
            held[lane, pl.ds(row, out_orders, stride=rows), :] = value[:, cut]
    for lane, cut in enumerate(lanes):
        out_ref[:, :, cut] = held[lane].reshape(out_orders, rows, LANES)


def finish(factors, before, pair_count, codes):
    rows, out_orders, cycles = before.shape
    factors = jnp.concatenate(factors, axis=1)
    high = lax.reduce_precision(factors, 8, 7)
    low = (factors - high).astype(jnp.bfloat16)
    high = high.astype(jnp.bfloat16)
    vmem = pl.BlockSpec(memory_space=pltpu.VMEM)
    return pl.pallas_call(
        finish_kernel,
        in_specs=[vmem] * (3 + len(codes)),
        out_specs=vmem,
        out_shape=jax.ShapeDtypeStruct((out_orders, rows, cycles), jnp.float32),
        scratch_shapes=[
            pltpu.VMEM((cycles // LANES, out_orders * rows, LANES), jnp.float32),
        ],
        compiler_params=pltpu.CompilerParams(vmem_limit_bytes=32 << 20),
    )(jnp.concatenate([high, high, low], axis=1), before, pair_count, *codes)


def swap(value, axis, size, shift):
    return lax.ppermute(value, axis, [(at, (at + shift) % size) for at in range(size)])


def at(value, index, axis=0):
    return lax.dynamic_index_in_dim(value, index, axis, keepdims=False)


def exchange(blocks, me, size):
    got = []
    for shift in range(size):
        block = at(blocks, me ^ shift)
        if shift:
            block = lax.ppermute(block, SNAP, [(dev, dev ^ shift) for dev in range(size)])
        got.append(block)
    return got


def compute(images, cycle_masks, weights, inversion):
    snap_dev, cycles, angles = images.shape
    orders = inversion.shape[0]
    low_size, x_size, core_size = (lax.axis_size(name) for name in GROUP)
    low, x_index, core_index = (lax.axis_index(name) for name in GROUP)
    ord_size = x_size * core_size
    snap_size = HALVES * low_size
    ord_index = x_index * core_size + core_index
    snap_index = lax.axis_index("high") * low_size + low
    group = low_size * ord_size
    owned = orders // group
    chunks = min(2, owned)
    part = owned // chunks
    rows = cycles // snap_size
    out_orders = orders // ord_size

    table = make_table(orders, angles).reshape(2, ord_size, low_size, chunks, part, angles)
    table = table.transpose(3, 2, 1, 0, 4, 5).reshape(2 * orders, angles)
    table = jnp.asarray(table).astype(jnp.bfloat16)

    first = jnp.reshape(ord_index * snap_dev, (1,)).astype(jnp.int32)
    coeffs = list(transform(first, table, cycle_masks, images, chunks, group))
    coeffs[0], cycle_masks, weights = lax.optimization_barrier((coeffs[0], cycle_masks, weights))
    arrived = []
    for chunk in range(chunks):
        block = coeffs[chunk].reshape(group, 2 * part * snap_dev, cycles)
        block = lax.all_to_all(block, GROUP, split_axis=0, concat_axis=0, tiled=True)
        block = (
            block.reshape(group, snap_dev, 2, part, cycles).transpose(0, 2, 3, 1, 4)
            if chunk < chunks - 1
            else block.reshape(group, 2, part, snap_dev, cycles)
        )
        arrived.append(block)

    masks = cycle_masks.astype(jnp.float32)
    counts = jnp.einsum("sq,sp->qp", masks * weights[:, None], masks, precision=lax.Precision.HIGHEST)
    weight_row = jnp.zeros((1, cycles), jnp.float32).at[0, : weights.shape[0]].set(weights)
    early = jnp.concatenate(
        [
            counts.reshape(snap_size, rows, cycles),
            jnp.broadcast_to(weight_row[None], (snap_size, 1, cycles)),
        ],
        axis=1,
    )
    blocks = exchange(early, snap_index, snap_size)
    pair_count = sum(block[:rows] for block in blocks)
    weight_half = jnp.stack([block[rows, : weights.shape[0]] for block in blocks[:low_size]])
    weight_half = jnp.stack([at(weight_half, low ^ k) for k in range(low_size)])
    weight_half = weight_half.reshape(group, snap_dev)

    own_rows = lax.dynamic_slice_in_dim(inversion, ord_index * out_orders, out_orders, 0)
    own_rows = own_rows.reshape(out_orders, x_size, core_size, low_size, chunks, part)

    def columns(chunk, x_from, core_from, crossed):
        picked = at(at(own_rows[:, :, :, :, chunk], x_from, 1), core_from, 1)
        if crossed:
            picked = jnp.stack([at(picked, low ^ k, 1) for k in range(low_size)], axis=1)
        return picked.reshape(out_orders, low_size * part)

    def contract(value, *place):
        return jnp.einsum("ln,nqp->qlp", columns(*place), value, precision=lax.Precision.HIGHEST)

    last_codes, last_factors = [], []
    total = 0.0
    for chunk in range(chunks):
        weighted = arrived[chunk].astype(jnp.float32) * weight_half[:, None, None, :, None]
        gram = jnp.einsum(
            "drnsq,drnsp->nqp",
            weighted.astype(jnp.bfloat16),
            arrived[chunk],
            preferred_element_type=jnp.float32,
        )
        gram = encode(gram).reshape(part, snap_size, rows, cycles).transpose(1, 0, 2, 3)
        crossed = chunk < chunks - 1
        if crossed:
            got = exchange(gram, snap_index, snap_size)
            gram = jnp.concatenate(
                [decode(got[k]) + decode(got[k + low_size]) for k in range(low_size)]
            )
        else:
            gram = lax.all_to_all(gram, SNAP, split_axis=0, concat_axis=0, tiled=True)
            gram = decode(gram).reshape(HALVES, low_size * part, rows, cycles).sum(0)
        code = encode(gram).transpose(1, 0, 2)
        total = total + contract(gram, chunk, x_index, core_index, crossed)
        for shift in range(x_size):
            x_from = (x_index - shift) % x_size
            seen = swap(code, "x", x_size, shift) if shift else code
            far = swap(seen, "core", core_size, 1)
            for piece, core_from in ((seen, core_index), (far, 1 - core_index)):
                place = (chunk, x_from, core_from, crossed)
                if shift and not crossed:
                    last_codes.append(piece)
                    last_factors.append(columns(*place))
                elif shift or core_from is not core_index:
                    total = total + contract((decode(piece).transpose(1, 0, 2) if piece is not gram else gram), *place)
    return finish(last_factors, total, pair_count, last_codes)


def solution(mesh):
    snap_size, ord_size = mesh.shape["snap"], mesh.shape["ord"]
    fine = Mesh(
        mesh.devices.reshape(HALVES, snap_size // HALVES, ord_size // 2, 2), SNAP + ORD
    )
    placed = (P(SNAP + ORD, None, None), P(SNAP, None), P(SNAP), P())
    return jax.shard_map(
        compute, mesh=fine, in_specs=placed, out_specs=P(ORD, SNAP, None), check_vma=False
    )
```
